32 devices in a mesh: px: 8 (over z, core), py: 4 (over y, x).
Axes of the slice: x: 2, y: 2, z: 4, core: 2. Of those that a mesh axis runs over, the one named last changes fastest.
Arguments:
- objective_grad: float32 [2, 8, 128, 512], P(None, None, 'px', 'py'), may hold values from -6 to 6
- coefficients: float32 [3, 128, 512], P(None, 'px', 'py'), may hold values from 0.2 to 2
- inv_x: bfloat16 [128, 4, 1, 128, 128], P('px', 'py'), may hold values from 0 to 1
- inv_y: bfloat16 [8, 16, 4, 128, 128], P('px', 'py'), may hold values from 0 to 1
- perf_cell: int32 [8192], P(('px', 'py')), may hold values from 0 to 2047
- perf_owner: int32 [8192, 1], P(('px', 'py')), may hold values from 0 to 3; in each aligned block of 256 rows (0 to 255, 256 to 511, ...) at most 128 rows name the same one
- perf_tile: float32 [2, 8192], P(None, ('px', 'py')), may hold values from -6 to 6
- perf_weight: float32 [8, 8192], P(None, ('px', 'py')), may hold values from -6 to 6
Outputs:
- adjoint: float32 [2, 8, 128, 512], P(None, None, 'px', 'py')
The draws below stay inside these ranges and needn't reach their ends.
Inputs may be any that keep to these rules, and one draw needn't show every extreme that they name: `perf_owner`: among the records of one block at most 128 name the same owner, and in some block one owner is named exactly 128 times.
All inputs are finite; a program needn't handle non-finite values.
Results may differ from the reference program's by a relative error of at most 0.00092.
Values may be sent and summed in bfloat16 or wider, within the bound.
A program may use at most 64 MiB of HBM per device.

```python
import math
import jax
import jax.numpy as jnp
import numpy as np
from jax import lax

CX = 16
CY = 128
SEGMENT = 128
OBJECTIVES = 8
REC_DEV = 256
NX = 128
NY = 512
CAP = 128
BAND = 1024
RECORDS = 8192
N_PX = 8
N_PY = 4


tail_reach = 0.075


tail_share = 0.68


diagonal_share = 0.3


jitter_spread = 0.75


def draw_fields(key):
    base = jax.random.fold_in(key, 11)
    storage = jnp.exp(jax.random.uniform(jax.random.fold_in(base, 1), (NX, NY), jnp.float32, math.log(0.5), math.log(2.0)))
    conduct_x = jnp.exp(jax.random.uniform(jax.random.fold_in(base, 2), (NX, NY), jnp.float32, math.log(0.2), math.log(2.0)))
    conduct_y = jnp.exp(jax.random.uniform(jax.random.fold_in(base, 3), (NX, NY), jnp.float32, math.log(0.2), math.log(2.0)))
    return (storage, conduct_x, conduct_y)


def diagonal_field(key):
    storage, conduct_x, conduct_y = draw_fields(key)
    lower_x = jnp.concatenate([jnp.zeros((1, NY), jnp.float32), conduct_x[:-1]], 0)
    lower_y = jnp.concatenate([jnp.zeros((NX, 1), jnp.float32), conduct_y[:, :-1]], 1)
    return storage + conduct_x + lower_x + conduct_y + lower_y


def kernel_shape():
    decay_rate = tail_reach ** (1.0 / SEGMENT)
    tail_weight = tail_share * (1.0 - decay_rate) / (2.0 * (1.0 - decay_rate ** (SEGMENT // 2)))
    positions = jnp.arange(SEGMENT).astype(jnp.float32)
    distance = jnp.abs(positions[:, None] - positions[None, :])
    on_diagonal = (distance == 0.0).astype(jnp.float32)
    return diagonal_share * on_diagonal + tail_weight * jnp.power(jnp.float32(decay_rate), distance)


def draw_objective_grad(key, part):
    full_shape = (2, OBJECTIVES, NX, NY)
    return jnp.clip(jax.random.normal(jax.random.fold_in(key, 32), full_shape, jnp.float32), -6.0, 6.0)


def draw_coefficients(key, part):
    storage, conduct_x, conduct_y = draw_fields(key)
    return jnp.stack([storage, conduct_x, conduct_y])


def draw_inv_x(key, part):
    diagonal = diagonal_field(key)
    arranged = diagonal.reshape(NX // SEGMENT, SEGMENT, NY // CY, CY).transpose(3, 2, 0, 1)
    jitter = jax.random.uniform(jax.random.fold_in(key, 21), (CY, NY // CY, NX // SEGMENT, SEGMENT, SEGMENT), jnp.float32, -1.0, 1.0)
    return (kernel_shape() * (1.0 + jitter_spread * jitter) / arranged[..., None]).astype(jnp.bfloat16)


def draw_inv_y(key, part):
    diagonal = diagonal_field(key)
    arranged = diagonal.reshape(NX // CX, CX, NY // SEGMENT, SEGMENT)
    jitter = jax.random.uniform(jax.random.fold_in(key, 22), (NX // CX, CX, NY // SEGMENT, SEGMENT, SEGMENT), jnp.float32, -1.0, 1.0)
    return (kernel_shape() * (1.0 + jitter_spread * jitter) / arranged[..., None]).astype(jnp.bfloat16)


def set_ends(array, key, low, top_value):
    dims = array.shape
    place = [jax.random.randint(jax.random.fold_in(key, axis), (), 0, dims[axis]) for axis in range(len(dims))]
    array = array.at[tuple(place)].set(low)
    longest = dims.index(max(dims))
    place[longest] = (place[longest] + 1) % dims[longest]
    return array.at[tuple(place)].set(top_value)


def block_scale(rng, extent, cuts, least, high):
    gain = 1.0
    for dim, shards_of in cuts:
        draws = jax.random.uniform(jax.random.fold_in(jax.random.fold_in(rng, 6), dim), (shards_of,), jnp.float32, least / len(cuts), high / len(cuts))
        gain = gain * jnp.repeat(jnp.exp(draws), extent[dim] // shards_of).reshape((-1,) + (1,) * (len(extent) - 1 - dim))
    return gain


def assign_block(stream_key, own, number, rows, number_of, top, limit, skew):
    sequence = jax.random.permutation(stream_key, number_of)
    crowded, usual = portions_of(number_of, rows * top, limit, skew, True), portions_of(number_of, rows * top, limit, skew, False)
    places = jnp.arange(number_of)

    def named(lengths, turn):
        used = int((lengths > 0).sum())
        fixed = max(1, used // 4)
        shifted = fixed + (places - fixed + turn * (used - fixed)) % max(1, number_of - fixed)
        return jnp.zeros((number_of,), jnp.int32).at[sequence[jnp.where(places < fixed, places, shifted)]].set(jnp.asarray(lengths, jnp.int32))

    lengths = jnp.where(number % 4 == 0, named(crowded, number // 4), named(usual, number - number // 4 - 1))
    mixed = jax.random.permutation(jax.random.fold_in(own, 3), number_of)
    giver, sink = mixed[0:number_of // 2 * 2:2], mixed[1:number_of // 2 * 2:2]
    margin = jnp.minimum(lengths[giver] - 1, limit - lengths[sink]) // 2
    margin = jnp.where((giver == sequence[0]) | (sink == sequence[0]) | (lengths[sink] == 0), 0, jnp.maximum(margin, 0))
    shifted = jax.random.randint(jax.random.fold_in(own, 4), (number_of // 2,), 0, 1 << 20) % (margin + 1)
    lengths = lengths.at[giver].add(-shifted).at[sink].add(shifted)
    labels = jnp.searchsorted(jnp.cumsum(lengths), jnp.arange(rows * top), side="right").astype(jnp.int32)
    table = labels.reshape(top, rows).T
    table = table[jax.random.permutation(jax.random.fold_in(own, 1), rows)]
    turn = jax.random.randint(jax.random.fold_in(own, 2), (rows, 1), 0, top)
    return jnp.take_along_axis(table, (jnp.arange(top)[None, :] + turn) % top, axis=1)


def portions_of(number_of, total, most, lean, full):
    portions = [(1 << 20) // math.isqrt(standing ** lean) + 1 for standing in range(1, number_of + 1)]
    largest = most if full else min(most, max(-(-total // number_of), total * portions[0] // sum(portions)))
    least = 1 if total - largest >= number_of - 1 else 0
    given, rest = [largest] + [least] * (number_of - 1), total - largest - least * (number_of - 1)
    while rest > 0:
        free = [i for i in range(1, number_of) if given[i] < largest] or [i for i in range(1, number_of) if given[i] < most]
        whole, budget = sum([portions[i] for i in free]), rest
        for i in free:
            more = min(most - given[i], max(1, budget * portions[i] // whole), rest)
            given[i] = given[i] + more
            rest = rest - more
    return np.array(given)


def bell_draw(own_key, dims, width, most, cuts=(), dtype=jnp.bfloat16):
    result = width * jax.random.normal(own_key, dims, jnp.float32)
    if cuts:
        result = result * block_scale(own_key, dims, cuts, -0.22, 0.18)
    return jnp.clip(result, -most, most).astype(dtype)


def setup_inputs(seed: int = 0) -> dict:
    streams_of = jax.random.split(jax.random.key(seed), 9)
    objective_grad = draw_objective_grad(jax.random.fold_in(streams_of[8], 71), 0)
    coefficients = draw_coefficients(jax.random.fold_in(streams_of[8], 71), 0)
    inv_x = draw_inv_x(jax.random.fold_in(streams_of[8], 71), 0)
    inv_y = draw_inv_y(jax.random.fold_in(streams_of[8], 71), 0)
    perf_cell = set_ends(jax.random.randint(streams_of[4], (RECORDS,), 0, CX * CY), jax.random.fold_in(streams_of[4], 1), 0, (CX * CY) - 1).astype(jnp.int32)
    perf_owner_keys = jax.random.split(jax.random.fold_in(streams_of[5], 1), RECORDS // REC_DEV)
    perf_owner_turns = jax.random.permutation(jax.random.fold_in(streams_of[5], 3), RECORDS // REC_DEV)
    perf_owner = jax.vmap(lambda own, number: assign_block(jax.random.fold_in(streams_of[5], 2), own, number, REC_DEV, N_PY, 1, CAP, 2))(perf_owner_keys, perf_owner_turns).reshape((RECORDS, 1))
    perf_tile = bell_draw(streams_of[6], (2, RECORDS), 1.0, 6.0, ((1, 32),), jnp.float32)
    perf_weight = bell_draw(streams_of[7], (OBJECTIVES, RECORDS), 1.0, 6.0, ((1, 32),), jnp.float32)
    return {"objective_grad": objective_grad, "coefficients": coefficients, "inv_x": inv_x, "inv_y": inv_y, "perf_cell": perf_cell, "perf_owner": perf_owner, "perf_tile": perf_tile, "perf_weight": perf_weight}


def operate(iterate, storage, conduct_x, conduct_y):
    lower_x = jnp.pad(conduct_x[:-1], ((1, 0), (0, 0)))
    lower_y = jnp.pad(conduct_y[:, :-1], ((0, 0), (1, 0)))
    diagonal = storage + conduct_x + lower_x + conduct_y + lower_y
    padded = jnp.pad(iterate, ((0, 0), (1, 1), (1, 1)))
    return (diagonal * iterate - conduct_x * padded[:, 2:, 1:-1] - lower_x * padded[:, :-2, 1:-1]
            - conduct_y * padded[:, 1:-1, 2:] - lower_y * padded[:, 1:-1, :-2])


def relax_first(residual, inv_x):
    rounded = residual.astype(jnp.bfloat16)

    def one_block(block_index):
        part_rows = lax.dynamic_slice_in_dim(rounded, block_index * CY, CY, 2)
        shaped = part_rows.reshape(OBJECTIVES, NX // SEGMENT, SEGMENT, CY).astype(jnp.float32)
        matrices = lax.dynamic_index_in_dim(inv_x, block_index, 1, keepdims=False).astype(jnp.float32)
        return jnp.einsum("ykij,qkjy->qkiy", matrices, shaped).reshape(OBJECTIVES, NX, CY)

    mapped = lax.map(one_block, jnp.arange(N_PY).astype(jnp.int32))
    return jnp.transpose(mapped, (1, 2, 0, 3)).reshape(OBJECTIVES, NX, NY)


def relax_second(residual, inv_y):
    rounded = residual.astype(jnp.bfloat16)

    def one_block(block_index):
        part_rows = lax.dynamic_slice_in_dim(rounded, block_index * CX, CX, 1)
        shaped = part_rows.reshape(OBJECTIVES, CX, NY // SEGMENT, SEGMENT).astype(jnp.float32)
        matrices = lax.dynamic_index_in_dim(inv_y, block_index, 0, keepdims=False).astype(jnp.float32)
        return jnp.einsum("xkij,qxkj->qxki", matrices, shaped).reshape(OBJECTIVES, CX, NY)

    mapped = lax.map(one_block, jnp.arange(N_PX).astype(jnp.int32))
    return jnp.transpose(mapped, (1, 0, 2, 3)).reshape(OBJECTIVES, NX, NY)


def reference(objective_grad, coefficients, inv_x, inv_y, perf_cell, perf_owner, perf_tile, perf_weight):
    storage = coefficients[0]
    conduct_x = coefficients[1]
    conduct_y = coefficients[2]

    def relaxed_solve(right_side):
        iterate = relax_first(right_side, inv_x)
        iterate = iterate + relax_second(right_side - operate(iterate, storage, conduct_x, conduct_y), inv_y)
        iterate = iterate + relax_first(right_side - operate(iterate, storage, conduct_x, conduct_y), inv_x)
        iterate = iterate + relax_second(right_side - operate(iterate, storage, conduct_x, conduct_y), inv_y)
        return iterate

    record_index = jnp.arange(RECORDS).astype(jnp.int32)
    band_index = record_index // BAND
    position_x = band_index * CX + perf_cell // CY
    position_y = perf_owner[:, 0] * CY + perf_cell % CY
    values = perf_tile[:, None, :] * perf_weight[None, :, :]
    well_loads = jnp.zeros((2, OBJECTIVES, NX, NY), jnp.float32).at[:, :, position_x, position_y].add(values)
    second_adjoint = relaxed_solve(objective_grad[1] + well_loads[1])
    first_adjoint = relaxed_solve((objective_grad[0] + well_loads[0]) + storage * second_adjoint)
    return jnp.stack([first_adjoint, second_adjoint])
```

```python
import functools

import jax
import jax.numpy as jnp
from jax import lax
from jax.experimental import pallas as pl
from jax.experimental.pallas import tpu as pltpu
from jax.sharding import PartitionSpec as P


def passed_along(value, axis, steps):
    count = lax.axis_size(axis)
    leading, last = (max(0, -steps), min(count, count - steps))
    return lax.ppermute(value, axis, [(source, source + steps) for source in range(leading, last)])


def extended(cells, sides, width):
    for axis, dim in sides:
        count = lax.axis_size(axis)
        ends = count - 1
        head = lax.slice_in_dim(cells, 0, width, axis=dim)
        tail = lax.slice_in_dim(cells, cells.shape[dim] - width, cells.shape[dim], axis=dim)
        cells = jnp.concatenate(
            [
                lax.ppermute(tail, axis, [(i, (i + 1) % count) for i in range(ends)]),
                cells,
                lax.ppermute(head, axis, [((i + 1) % count, i) for i in range(ends)]),
            ],
            axis=dim,
        )
    return cells


def shards(
    objective_grad, coefficients, inv_x, inv_y, perf_cell, perf_owner, perf_tile, perf_weight
):
    objectives = objective_grad.shape[1]
    width_x = coefficients.shape[1]
    width_y = coefficients.shape[2]
    storage = coefficients[0]
    conduct_x = coefficients[1]
    conduct_y = coefficients[2]
    below_x = passed_along(conduct_x[-1:, :], "px", 1)
    below_y = passed_along(conduct_y[:, -1:], "py", 1)
    lower_x = jnp.concatenate([below_x, conduct_x[:-1, :]], 0)
    lower_y = jnp.concatenate([below_y, conduct_y[:, :-1]], 1)
    diagonal = storage + conduct_x + lower_x + conduct_y + lower_y
    segment = inv_x.shape[3]
    blocks_x = inv_x.reshape(inv_x.shape[0], inv_x.shape[2], segment, segment)
    blocks_y = inv_y.reshape(inv_y.shape[1], inv_y.shape[2], segment, segment)

    def operate(iterate):
        padded = extended(iterate, (("px", 1), ("py", 2)), 1)
        return (
            diagonal * iterate
            - conduct_x * padded[:, 2:, 1:-1]
            - lower_x * padded[:, :-2, 1:-1]
            - conduct_y * padded[:, 1:-1, 2:]
            - lower_y * padded[:, 1:-1, :-2]
        )

    def relax_first(residual):
        turned = jnp.swapaxes(residual.astype(jnp.bfloat16), 1, 2)
        line_rows = lax.all_to_all(turned, "px", split_axis=1, concat_axis=2, tiled=True)
        shaped = line_rows.reshape(objectives, line_rows.shape[1], -1, segment)
        update = jnp.einsum("rkij,qrkj->qrki", blocks_x, shaped, preferred_element_type=jnp.float32)
        returned = lax.all_to_all(
            update.reshape(line_rows.shape), "px", split_axis=2, concat_axis=1, tiled=True
        )
        return jnp.swapaxes(returned, 1, 2)

    def relax_second(residual):
        line_rows = lax.all_to_all(
            residual.astype(jnp.bfloat16), "py", split_axis=1, concat_axis=2, tiled=True
        )
        shaped = line_rows.reshape(objectives, line_rows.shape[1], -1, segment)
        update = jnp.einsum("xkij,qxkj->qxki", blocks_y, shaped, preferred_element_type=jnp.float32)
        return lax.all_to_all(
            update.reshape(line_rows.shape), "py", split_axis=2, concat_axis=1, tiled=True
        )

    def relaxed_solve(right_side):
        iterate = relax_first(right_side)
        iterate = iterate + relax_second(right_side - operate(iterate))
        iterate = iterate + relax_first(right_side - operate(iterate))
        iterate = iterate + relax_second(right_side - operate(iterate))
        return iterate

    records = perf_cell.shape[0]
    owners = lax.axis_size("py")
    capacity = 2 * records // owners
    payload = jnp.concatenate([perf_tile, perf_weight, perf_cell.astype(jnp.float32)[None, :]], 0)
    owner_index = perf_owner[:, 0]
    onehot = (owner_index[:, None] == jnp.arange(owners, dtype=jnp.int32)[None, :]).astype(
        jnp.int32
    )
    rank_in_owner = jnp.sum((jnp.cumsum(onehot, 0) - 1) * onehot, axis=1)
    slot_index = owner_index * capacity + rank_in_owner
    packed = (
        jnp.zeros((payload.shape[0], owners * capacity), jnp.float32).at[:, slot_index].set(payload)
    )
    arrived = lax.all_to_all(packed, "py", split_axis=1, concat_axis=1, tiled=True)
    tile_rows = arrived[0:2]
    weight_rows = arrived[2 : 2 + objectives]
    cell_index = arrived[2 + objectives].astype(jnp.int32)
    values = tile_rows[:, None, :] * weight_rows[None, :, :]
    well_loads = (
        jnp.zeros((2, objectives, width_x * width_y), jnp.float32).at[:, :, cell_index].add(values)
    )
    well_loads = well_loads.reshape(2, objectives, width_x, width_y)
    second_adjoint = relaxed_solve(objective_grad[1] + well_loads[1])
    first_adjoint = relaxed_solve(objective_grad[0] + well_loads[0] + storage * second_adjoint)
    return jnp.stack([first_adjoint, second_adjoint])


MESH = pl.DeviceIdType.MESH
DIAG, COND_X, LOW_X, COND_Y, LOW_Y, STORE = range(6)
B_TO_LINES, Z1_TO_CELLS, Z2_TO_LINES, Z3_TO_CELLS = range(4)
COEF = 8


def swap_bits(tiles, tile_bit, shift, lane):
    keep = (lane & shift) == 0
    width = lane.shape[1]
    out = list(tiles)
    for a in range(len(tiles)):
        if a & tile_bit:
            continue
        b = a | tile_bit
        out[a] = jnp.where(keep, tiles[a], pltpu.roll(tiles[b], shift, 1))
        out[b] = jnp.where(keep, pltpu.roll(tiles[a], width - shift, 1), tiles[b])
    return out


def fused(
    n_px, n_py, cells_x,
    grad, coef, inv_x, inv_y, cell, owner, tile, weight,
    out,
    sent, got, sent_far, lines_far, cells_far, records, near_x, near_y, coef_cells, coef_lines, blocks_y, loads,
    grad_here, coef_here, blocks_x, cell_here, owner_here, tile_here,
    send_sem, recv_sem, far_send, far_recv, rec_send, rec_recv, near_send, near_recv, inv_send, inv_recv, inv_own, load_sem,
):
    me = lax.axis_index("px")
    mk = lax.axis_index("py")
    after_k, before_k = lax.rem(mk + 1, n_py), lax.rem(mk + n_py - 1, n_py)
    objectives, width = weight.shape[0], coef.shape[2]
    parts = cells_x // n_px
    last = cells_x - 1
    per_y = inv_y.shape[0]
    lane = lax.broadcasted_iota(jnp.int32, (objectives, width), 1)
    group = lane // cells_x
    sub = lax.broadcasted_iota(jnp.int32, (objectives, width), 0)

    def remote(source, target, sems, where):
        return pltpu.make_async_remote_copy(
            src_ref=source, dst_ref=target, send_sem=sems[0], recv_sem=sems[1],
            device_id=where, device_id_type=MESH,
        )

    def await_bytes(ref, sem):
        pltpu.make_async_copy(ref, ref, sem).wait()

    def swap_axes(tiles):
        bit = 1
        while bit < cells_x:
            tiles = swap_bits(tiles, bit, bit, lane)
            bit *= 2
        return tiles

    def swap_blocks(tiles):
        bit = 1
        while bit < n_px:
            tiles = swap_bits(tiles, bit, bit * cells_x, lane)
            bit *= 2
        return tiles

    def shifted(value, groups):
        amount = (groups * cells_x) % width
        return value if amount == 0 else pltpu.roll(value, amount, 1)

    def swap_rows(value, lane_bit, row_bit):
        low_lane, low_row = (lane & lane_bit) == 0, (sub & row_bit) == 0
        onward = pltpu.roll(pltpu.roll(value, row_bit, 0), width - lane_bit, 1)
        backward = pltpu.roll(pltpu.roll(value, objectives - row_bit, 0), lane_bit, 1)
        return jnp.where(low_lane == low_row, value, jnp.where(low_row, backward, onward))

    def turn_edges(up, down):
        pair = swap_bits([up, down], 1, cells_x, lane)
        return [swap_rows(swap_rows(t, 4 * cells_x, 4), 2 * cells_x, 2) for t in pair]

    def peers():
        low = me < n_px // 2
        for i in range(n_px - 1):
            down, up = n_px - 1 - i, i
            down = jnp.where(down <= me, down - 1, down)
            up = jnp.where(up >= me, up + 1, up)
            yield jnp.where(low, down, up)

    full = parts * objectives

    def rows_of(edges):
        return pl.ds(0, full + 2 if edges else full)

    def send(phase, tiles, edges, to_lines):
        turned = swap_axes(tiles)
        packed = swap_blocks(turned)
        for p in range(n_px):
            for part in range(parts):
                sent[phase, p, pl.ds(part * objectives, objectives)] = packed[part * n_px + p]
        if edges:
            up = jnp.where(group == 0, 0.0, shifted(turned[last], 1))
            down = jnp.where(group == n_px - 1, 0.0, shifted(turned[0], -1))
            pair = turn_edges(up, down)
            for p in range(n_px):
                row = p // 2 * 2
                sent[phase, p, pl.ds(full, 2)] = pair[p % 2][row : row + 2]
            if to_lines:
                sent_far[phase, 0] = pltpu.roll(turned[last], lax.rem(me + 1, n_px) * cells_x, 1)
                sent_far[phase, 1] = pltpu.roll(turned[0], me * cells_x, 1)
            else:
                sent_far[phase, 0] = tiles[last]
                sent_far[phase, 1] = tiles[0]
            for copies, here in far_copies(phase, to_lines):
                @pl.when(here)
                def _():
                    for copy in copies:
                        copy.start()
        rows = rows_of(edges)
        for to in peers():
            remote(
                sent.at[phase, to, rows], got.at[phase, me, rows],
                (send_sem.at[phase], recv_sem.at[phase]), (to, mk),
            ).start()
        got[phase, me, rows] = sent[phase, me, rows]

    def far_copies(phase, to_lines):
        index = phase // 2
        copies = []
        sems = [(far_send.at[phase, d], far_recv.at[phase, d]) for d in range(2)]
        if to_lines:
            copies.append(([remote(sent_far.at[phase, 0], lines_far.at[index, 0, me], sems[0], (0, after_k))], mk + 1 < n_py))
            copies.append(([remote(sent_far.at[phase, 1], lines_far.at[index, 1, me], sems[1], (n_px - 1, before_k))], mk > 0))
        else:
            copies.append((
                [remote(sent_far.at[phase, 0], cells_far.at[index, 0], sems[0], (d, after_k)) for d in range(n_px)],
                (me == n_px - 1) & (mk + 1 < n_py),
            ))
            copies.append((
                [remote(sent_far.at[phase, 1], cells_far.at[index, 1], sems[1], (d, before_k)) for d in range(n_px)],
                (me == 0) & (mk > 0),
            ))
        return copies

    def receive(phase, edges, to_lines):
        await_bytes(got.at[phase, pl.ds(0, n_px - 1), rows_of(edges)], recv_sem.at[phase])
        tiles = swap_blocks(
            [got[phase, p, pl.ds(part * objectives, objectives)] for part in range(parts) for p in range(n_px)]
        )
        if not edges:
            return tiles
        up, down = turn_edges(
            *[
                jnp.concatenate([got[phase, p, pl.ds(full, 2)] for p in range(first, n_px, 2)], 0)
                for first in range(2)
            ]
        )
        index = phase // 2
        if to_lines:
            @pl.when((me == 0) & (mk > 0))
            def _():
                await_bytes(lines_far.at[index, 0], far_recv.at[phase, 0])

            @pl.when((me == n_px - 1) & (mk + 1 < n_py))
            def _():
                await_bytes(lines_far.at[index, 1], far_recv.at[phase, 1])

            far = []
            for d in range(2):
                value = lines_far[index, d, 0]
                for p in range(1, n_px):
                    value = jnp.where(group == p, lines_far[index, d, p], value)
                far.append(value)
            return tiles, up + far[0], down + far[1], None, None

        @pl.when(mk > 0)
        def _():
            await_bytes(cells_far.at[index, 0], far_recv.at[phase, 0])

        @pl.when(mk + 1 < n_py)
        def _():
            await_bytes(cells_far.at[index, 1], far_recv.at[phase, 1])

        back = lax.rem(n_px - me, n_px) * cells_x
        left = pltpu.roll(cells_far[index, 0], back, 1)
        right = pltpu.roll(cells_far[index, 1], back, 1)
        lefts = [left if x == 0 else pltpu.roll(left, width - x, 1) for x in range(cells_x)]
        rights = [pltpu.roll(right, width - 1 - x, 1) for x in range(cells_x)]
        return tiles, up, down, lefts, rights

    def residual(right_side, field, coefs, tile_next, tile_prev, lane_next, lane_prev):
        tiles, up, down, lefts, rights = field
        result = []
        for t in range(cells_x):
            z = tiles[t]
            before = up if t == 0 else tiles[t - 1]
            after = down if t == last else tiles[t + 1]
            left = jnp.where(lane == 0, 0.0 if lefts is None else lefts[t], pltpu.roll(z, 1, 1))
            right = jnp.where(lane == width - 1, 0.0 if rights is None else rights[t], pltpu.roll(z, width - 1, 1))

            def c(row):
                return coefs[t, pl.ds(row, 1), :]

            applied = c(DIAG) * z - c(tile_next) * after - c(tile_prev) * before - c(lane_next) * right - c(lane_prev) * left
            result.append(right_side[t] - applied)
        return result

    def relax(blocks, res):
        return [
            lax.dot_general(
                res[t].astype(jnp.bfloat16), blocks[t], (((1,), (1,)), ((), ())),
                preferred_element_type=jnp.float32,
            )
            for t in range(cells_x)
        ]

    barrier = pltpu.get_barrier_semaphore()
    for to in peers():
        pl.semaphore_signal(barrier, inc=1, device_id=(to, mk), device_id_type=MESH)
    for d in range(1, n_py):
        pl.semaphore_signal(barrier, inc=1, device_id=(me, lax.rem(mk + d, n_py)), device_id_type=MESH)

    pairs = (
        (weight, records.at[mk, pl.ds(0, objectives)]), (tile, tile_here), (cell, cell_here), (owner, owner_here),
        (coef, coef_here), (grad, grad_here), (inv_x, blocks_x),
    )
    fetches = [pltpu.make_async_copy(*pair, load_sem.at[i]) for i, pair in enumerate(pairs)]
    for fetch in fetches:
        fetch.start()
    own_blocks = pltpu.make_async_copy(inv_y.at[:, mk], blocks_y.at[pl.ds(mk * per_y, per_y)], inv_own)
    own_blocks.start()
    lines_far[...] = jnp.zeros_like(lines_far)
    cells_far[...] = jnp.zeros_like(cells_far)

    def record_copy(d):
        return remote(records.at[mk], records.at[mk], (rec_send, rec_recv), (me, lax.rem(mk + d, n_py)))

    def block_copy(d):
        to = lax.rem(mk + d, n_py)
        return remote(
            inv_y.at[:, to], blocks_y.at[pl.ds(mk * per_y, per_y)], (inv_send, inv_recv), (me, to)
        )

    copy_x = remote(coef_here.at[1], near_x, (near_send.at[0], near_recv.at[0]), (lax.rem(me + 1, n_px), mk))
    copy_y = remote(coef_here.at[2], near_y, (near_send.at[1], near_recv.at[1]), (me, after_k))
    has_x, has_y = me + 1 < n_px, mk + 1 < n_py

    count = weight.shape[1]
    span = cells_x * objectives
    x_number = lax.broadcasted_iota(jnp.int32, (cells_x, objectives, count), 0).astype(jnp.float32)
    y_number = lax.broadcasted_iota(jnp.int32, (width, count), 0).astype(jnp.float32)

    def loads_from(source, s):
        cells = records[source, pl.ds(objectives + 2, 1)]
        owners = records[source, pl.ds(objectives + 3, 1)]
        at_x = jnp.floor(cells * (1.0 / width))
        at_y = cells - at_x * width
        at_x = jnp.where(owners == mk.astype(jnp.float32), at_x, -1.0)
        hit = x_number == at_x[None]
        spread = (y_number == at_y).astype(jnp.float32).astype(jnp.bfloat16)
        value = records[source, pl.ds(objectives + s, 1)] * records[source, pl.ds(0, objectives)]
        high = value.astype(jnp.bfloat16).astype(jnp.float32)
        rows = [
            jnp.where(hit, piece[None], 0.0).reshape(span, count).astype(jnp.bfloat16)
            for piece in (high, value - high)
        ]
        total = lax.dot_general(
            jnp.concatenate(rows, 0), spread, (((1,), (1,)), ((), ())), preferred_element_type=jnp.float32
        )
        return total[:span] + total[span:]

    for fetch in fetches[:4]:
        fetch.wait()
    records[mk, pl.ds(objectives, 2)] = tile_here[...]
    records[mk, pl.ds(objectives + 2, 1)] = cell_here[...].astype(jnp.float32)
    records[mk, pl.ds(objectives + 3, 1)] = owner_here[...].astype(jnp.float32)
    fetches[4].wait()
    for s in range(2):
        loads[s] = loads_from(mk, s)
    pl.semaphore_wait(barrier, n_px + n_py - 2)
    for d in range(1, n_py):
        record_copy(d).start()
    pl.when(has_x)(lambda: copy_x.start())
    pl.when(has_y)(lambda: copy_y.start())
    fetches[5].wait()
    fetches[6].wait()
    await_bytes(records.at[pl.ds(0, n_py - 1)], rec_recv)

    def add_loads(s):
        total = loads[s]
        for d in range(1, n_py):
            total = total + loads_from(lax.rem(mk + d, n_py), s)
        loads[s] = total

    add_loads(1)

    def loaded(s):
        return [
            grad_here[s, :, t, :] + loads[s, pl.ds(t * objectives, objectives), :]
            for t in range(cells_x)
        ]

    def solve(base, right_side):
        send(base + B_TO_LINES, right_side, False, True)
        if base == 0:
            for step in range(1, n_py):
                block_copy(step).start()
            share_coefficients()
            add_loads(0)
        line_side = receive(base + B_TO_LINES, False, True)
        send(base + Z1_TO_CELLS, relax(blocks_x, line_side), True, False)
        field = receive(base + Z1_TO_CELLS, True, False)
        res = residual(right_side, field, coef_cells, COND_X, LOW_X, COND_Y, LOW_Y)
        if base == 0:
            await_bytes(blocks_y.at[pl.ds(0, per_y * (n_py - 1))], inv_recv)
            own_blocks.wait()
        update = relax(blocks_y, res)
        send(base + Z2_TO_LINES, [z + u for z, u in zip(field[0], update)], True, True)
        field = receive(base + Z2_TO_LINES, True, True)
        if base == 0:
            for t, value in enumerate(receive(COEF, False, True)):
                coef_lines[t] = value
        update = relax(blocks_x, residual(line_side, field, coef_lines, COND_Y, LOW_Y, COND_X, LOW_X))
        send(base + Z3_TO_CELLS, [z + u for z, u in zip(field[0], update)], True, False)
        field = receive(base + Z3_TO_CELLS, True, False)
        update = relax(blocks_y, residual(right_side, field, coef_cells, COND_X, LOW_X, COND_Y, LOW_Y))
        return [z + u for z, u in zip(field[0], update)]

    def share_coefficients():
        storage, conduct_x, conduct_y = coef_here[0], coef_here[1], coef_here[2]
        pl.when(me > 0)(lambda: await_bytes(near_x, near_recv.at[0]))
        pl.when(mk > 0)(lambda: await_bytes(near_y, near_recv.at[1]))
        row = lax.broadcasted_iota(jnp.int32, conduct_x.shape, 0)
        column = lax.broadcasted_iota(jnp.int32, conduct_x.shape, 1)
        below_x = jnp.where(me > 0, pltpu.roll(near_x[...], 1, 0), 0.0)
        below_y = jnp.where(mk > 0, pltpu.roll(near_y[...], 1, 1), 0.0)
        lower_x = jnp.where(row == 0, below_x, pltpu.roll(conduct_x, 1, 0))
        lower_y = jnp.where(column == 0, below_y, pltpu.roll(conduct_y, 1, 1))
        diagonal = storage + conduct_x + lower_x + conduct_y + lower_y
        tiles = []
        for t in range(cells_x):
            value = jnp.zeros((objectives, width), jnp.float32)
            for number, array in enumerate((diagonal, conduct_x, lower_x, conduct_y, lower_y, storage)):
                value = jnp.where(sub == number, array[t : t + 1], value)
            coef_cells[t] = value
            tiles.append(value)
        send(COEF, tiles, False, True)

    def keep(s, tiles):
        for t in range(cells_x):
            out[s, :, t, :] = tiles[t]

    second = solve(0, loaded(1))
    keep(1, second)
    first_side = [b + coef_cells[t, pl.ds(STORE, 1), :] * second[t] for t, b in enumerate(loaded(0))]
    keep(0, solve(4, first_side))

    for phase in range(9):
        edges = phase != COEF and phase % 4 != B_TO_LINES
        await_bytes(sent.at[phase, pl.ds(0, n_px - 1), rows_of(edges)], send_sem.at[phase])
        if edges:
            for copies, here in far_copies(phase, phase % 4 == Z2_TO_LINES):
                @pl.when(here)
                def _():
                    for copy in copies:
                        copy.wait_send()
    await_bytes(records.at[pl.ds(0, n_py - 1)], rec_send)
    await_bytes(blocks_y.at[pl.ds(0, per_y * (n_py - 1))], inv_send)
    pl.when(has_x)(lambda: copy_x.wait_send())
    pl.when(has_y)(lambda: copy_y.wait_send())


def fused_shards(
    objective_grad, coefficients, inv_x, inv_y, perf_cell, perf_owner, perf_tile, perf_weight
):
    steps, objectives, cells_x, width = objective_grad.shape
    n_px, n_py = lax.axis_size("px"), lax.axis_size("py")
    segment = inv_x.shape[3]
    records = perf_cell.shape[0]
    parts = cells_x // n_px
    f32 = jnp.float32
    dma = pltpu.SemaphoreType.DMA
    vmem = pl.BlockSpec(memory_space=pltpu.VMEM)
    anywhere = pl.BlockSpec(memory_space=pl.ANY)
    tile = (objectives, width)
    result = pl.pallas_call(
        functools.partial(fused, n_px, n_py, cells_x),
        out_shape=pltpu.VMEM(objective_grad.shape, f32),
        in_specs=[anywhere] * 8,
        out_specs=vmem,
        scratch_shapes=[
            pltpu.VMEM((9, n_px, (parts + 1) * objectives, width), f32),
            pltpu.VMEM((9, n_px, (parts + 1) * objectives, width), f32),
            pltpu.VMEM((8, 2) + tile, f32),
            pltpu.VMEM((4, 2, n_px) + tile, f32),
            pltpu.VMEM((4, 2) + tile, f32),
            pltpu.VMEM((n_py, 2 * objectives, records), f32),
            pltpu.VMEM((cells_x, width), f32),
            pltpu.VMEM((cells_x, width), f32),
            pltpu.VMEM((cells_x,) + tile, f32),
            pltpu.VMEM((cells_x,) + tile, f32),
            pltpu.VMEM((cells_x, segment, segment), jnp.bfloat16),
            pltpu.VMEM((steps, objectives * cells_x, width), f32),
            pltpu.VMEM(objective_grad.shape, f32),
            pltpu.VMEM(coefficients.shape, f32),
            pltpu.VMEM((cells_x, segment, segment), jnp.bfloat16),
            pltpu.VMEM((1, records), jnp.int32),
            pltpu.VMEM((1, records), jnp.int32),
            pltpu.VMEM((2, records), f32),
            dma((9,)), dma((9,)), dma((8, 2)), dma((8, 2)),
            dma, dma, dma((2,)), dma((2,)), dma, dma, dma, dma((7,)),
        ],
        compiler_params=pltpu.CompilerParams(collective_id=0, has_side_effects=True),
    )(
        objective_grad,
        coefficients,
        inv_x.reshape(inv_x.shape[0], segment, segment),
        inv_y.reshape(inv_y.shape[1:]),
        perf_cell.reshape(1, records),
        perf_owner.reshape(1, records),
        perf_tile,
        perf_weight,
    )
    return result


def per_device(*args):
    grad, inv_x = args[0], args[2]
    objectives, cells_x, width = grad.shape[1:]
    n_px = lax.axis_size("px")
    fits = (
        inv_x.shape[2] == 1
        and width == inv_x.shape[3] == 128
        and cells_x * n_px == width
        and inv_x.shape[0] == cells_x
        and cells_x % n_px == 0
        and n_px == objectives == 8
    )
    return fused_shards(*args) if fits else shards(*args)


def solution(mesh):
    return jax.shard_map(
        per_device,
        mesh=mesh,
        in_specs=(
            P(None, None, "px", "py"),
            P(None, "px", "py"),
            P("px", "py", None, None, None),
            P("px", "py", None, None, None),
            P(("px", "py")),
            P(("px", "py"), None),
            P(None, ("px", "py")),
            P(None, ("px", "py")),
        ),
        out_specs=P(None, None, "px", "py"),
        check_vma=False,
    )
```

```python
import functools

import jax
import jax.numpy as jnp
from jax import lax
from jax.experimental import pallas as pl
from jax.experimental.pallas import tpu as pltpu
from jax.sharding import PartitionSpec as P


def passed_along(value, axis, steps):
    count = lax.axis_size(axis)
    leading, last = (max(0, -steps), min(count, count - steps))
    return lax.ppermute(value, axis, [(source, source + steps) for source in range(leading, last)])


def extended(cells, sides, width):
    for axis, dim in sides:
        count = lax.axis_size(axis)
        ends = count - 1
        head = lax.slice_in_dim(cells, 0, width, axis=dim)
        tail = lax.slice_in_dim(cells, cells.shape[dim] - width, cells.shape[dim], axis=dim)
        cells = jnp.concatenate(
            [
                lax.ppermute(tail, axis, [(i, (i + 1) % count) for i in range(ends)]),
                cells,
                lax.ppermute(head, axis, [((i + 1) % count, i) for i in range(ends)]),
            ],
            axis=dim,
        )
    return cells


def shards(
    objective_grad, coefficients, inv_x, inv_y, perf_cell, perf_owner, perf_tile, perf_weight
):
    objectives = objective_grad.shape[1]
    width_x = coefficients.shape[1]
    width_y = coefficients.shape[2]
    storage = coefficients[0]
    conduct_x = coefficients[1]
    conduct_y = coefficients[2]
    below_x = passed_along(conduct_x[-1:, :], "px", 1)
    below_y = passed_along(conduct_y[:, -1:], "py", 1)
    lower_x = jnp.concatenate([below_x, conduct_x[:-1, :]], 0)
    lower_y = jnp.concatenate([below_y, conduct_y[:, :-1]], 1)
    diagonal = storage + conduct_x + lower_x + conduct_y + lower_y
    segment = inv_x.shape[3]
    blocks_x = inv_x.reshape(inv_x.shape[0], inv_x.shape[2], segment, segment)
    blocks_y = inv_y.reshape(inv_y.shape[1], inv_y.shape[2], segment, segment)

    def operate(iterate):
        padded = extended(iterate, (("px", 1), ("py", 2)), 1)
        return (
            diagonal * iterate
            - conduct_x * padded[:, 2:, 1:-1]
            - lower_x * padded[:, :-2, 1:-1]
            - conduct_y * padded[:, 1:-1, 2:]
            - lower_y * padded[:, 1:-1, :-2]
        )

    def relax_first(residual):
        turned = jnp.swapaxes(residual.astype(jnp.bfloat16), 1, 2)
        line_rows = lax.all_to_all(turned, "px", split_axis=1, concat_axis=2, tiled=True)
        shaped = line_rows.reshape(objectives, line_rows.shape[1], -1, segment)
        update = jnp.einsum("rkij,qrkj->qrki", blocks_x, shaped, preferred_element_type=jnp.float32)
        returned = lax.all_to_all(
            update.reshape(line_rows.shape), "px", split_axis=2, concat_axis=1, tiled=True
        )
        return jnp.swapaxes(returned, 1, 2)

    def relax_second(residual):
        line_rows = lax.all_to_all(
            residual.astype(jnp.bfloat16), "py", split_axis=1, concat_axis=2, tiled=True
        )
        shaped = line_rows.reshape(objectives, line_rows.shape[1], -1, segment)
        update = jnp.einsum("xkij,qxkj->qxki", blocks_y, shaped, preferred_element_type=jnp.float32)
        return lax.all_to_all(
            update.reshape(line_rows.shape), "py", split_axis=2, concat_axis=1, tiled=True
        )

    def relaxed_solve(right_side):
        iterate = relax_first(right_side)
        iterate = iterate + relax_second(right_side - operate(iterate))
        iterate = iterate + relax_first(right_side - operate(iterate))
        iterate = iterate + relax_second(right_side - operate(iterate))
        return iterate

    records = perf_cell.shape[0]
    owners = lax.axis_size("py")
    capacity = 2 * records // owners
    payload = jnp.concatenate([perf_tile, perf_weight, perf_cell.astype(jnp.float32)[None, :]], 0)
    owner_index = perf_owner[:, 0]
    onehot = (owner_index[:, None] == jnp.arange(owners, dtype=jnp.int32)[None, :]).astype(
        jnp.int32
    )
    rank_in_owner = jnp.sum((jnp.cumsum(onehot, 0) - 1) * onehot, axis=1)
    slot_index = owner_index * capacity + rank_in_owner
    packed = (
        jnp.zeros((payload.shape[0], owners * capacity), jnp.float32).at[:, slot_index].set(payload)
    )
    arrived = lax.all_to_all(packed, "py", split_axis=1, concat_axis=1, tiled=True)
    tile_rows = arrived[0:2]
    weight_rows = arrived[2 : 2 + objectives]
    cell_index = arrived[2 + objectives].astype(jnp.int32)
    values = tile_rows[:, None, :] * weight_rows[None, :, :]
    well_loads = (
        jnp.zeros((2, objectives, width_x * width_y), jnp.float32).at[:, :, cell_index].add(values)
    )
    well_loads = well_loads.reshape(2, objectives, width_x, width_y)
    second_adjoint = relaxed_solve(objective_grad[1] + well_loads[1])
    first_adjoint = relaxed_solve(objective_grad[0] + well_loads[0] + storage * second_adjoint)
    return jnp.stack([first_adjoint, second_adjoint])


MESH = pl.DeviceIdType.MESH
DIAG, COND_X, LOW_X, COND_Y, LOW_Y, STORE = range(6)
B_TO_LINES, Z1_TO_CELLS, Z2_TO_LINES, Z3_TO_CELLS = range(4)
COEF = 8


def skewed_swap(tiles, step, lane):
    count, width = len(tiles), lane.shape[1]
    digit = (lane // step) % count
    moved = [t if i == 0 else pltpu.roll(t, i * step % width, 1) for i, t in enumerate(tiles)]
    out = [moved[-i % count] for i in range(count)]
    bit = 1
    while bit < count:
        on = (digit & bit) != 0
        out = [jnp.where(on, out[(i - bit) % count], out[i]) for i in range(count)]
        bit *= 2
    return out


def fused(
    n_px, n_py, cells_x,
    grad, coef, inv_x, inv_y, cell, owner, tile, weight,
    out,
    sent, got, sent_far, lines_far, cells_far, records, near_x, near_y, coef_cells, coef_lines, blocks_y, loads,
    grad_here, coef_here, blocks_x, cell_here, owner_here, tile_here,
    send_sem, recv_sem, far_send, far_recv, rec_send, rec_recv, near_send, near_recv, inv_send, inv_recv, inv_own, load_sem,
):
    me = lax.axis_index("px")
    mk = lax.axis_index("py")
    after_k, before_k = lax.rem(mk + 1, n_py), lax.rem(mk + n_py - 1, n_py)
    objectives, width = weight.shape[0], coef.shape[2]
    parts = cells_x // n_px
    last = cells_x - 1
    per_y = inv_y.shape[0]
    lane = lax.broadcasted_iota(jnp.int32, (objectives, width), 1)
    group = lane // cells_x
    digit = lane % n_px
    ring = lane // n_px
    sub = lax.broadcasted_iota(jnp.int32, (objectives, width), 0)

    def remote(source, target, sems, where):
        return pltpu.make_async_remote_copy(
            src_ref=source, dst_ref=target, send_sem=sems[0], recv_sem=sems[1],
            device_id=where, device_id_type=MESH,
        )

    def await_bytes(ref, sem):
        pltpu.make_async_copy(ref, ref, sem).wait()

    def rolled(value, amount):
        return value if amount % width == 0 else pltpu.roll(value, amount % width, 1)

    def exchanged(tiles, step):
        return [rolled(t, -i * step) for i, t in enumerate(skewed_swap(tiles, step, lane))]

    def peers():
        low = me < n_px // 2
        for i in range(n_px - 1):
            down, up = n_px - 1 - i, i
            down = jnp.where(down <= me, down - 1, down)
            up = jnp.where(up >= me, up + 1, up)
            yield jnp.where(low, down, up)

    full = 2 * parts * objectives

    def rows_of(edges):
        return pl.ds(0, full + objectives if edges else full)

    def send(phase, tiles, edges, to_lines):
        zero = jnp.zeros((objectives, width), jnp.float32)
        borders = None
        if to_lines:
            turned = exchanged(tiles, n_px)
            packed = [[turned[parts * p + i] for i in range(parts)] for p in range(n_px)]
            if edges:
                borders = [
                    jnp.where(
                        digit == n_px - 1,
                        zero if p == 0 else packed[p - 1][parts - 1],
                        zero if p == n_px - 1 else packed[p + 1][0],
                    )
                    for p in range(n_px)
                ]
                sent_far[phase, 0] = turned[last]
                sent_far[phase, 1] = turned[0]
        else:
            halves = [skewed_swap(tiles[i * n_px : (i + 1) * n_px], 1, lane) for i in range(parts)]
            packed = [[rolled(halves[i][p], -p) for i in range(parts)] for p in range(n_px)]
            borders = []
            for p in range(n_px):
                value = zero
                if p > 0:
                    high = jnp.where(
                        ring == cells_x - 1, packed[p - 1][1], rolled(halves[0][p - 1], -(p - 1) - n_px)
                    )
                    value = jnp.where(ring >= cells_x - 2, high, value)
                if p < n_px - 1:
                    low = jnp.where(ring == 0, packed[p + 1][0], rolled(halves[1][p + 1], n_px - (p + 1)))
                    value = jnp.where(ring <= 1, low, value)
                borders.append(value)
            sent_far[phase, 0] = tiles[last]
            sent_far[phase, 1] = tiles[0]
        for p in range(n_px):
            value = jnp.concatenate(packed[p], 0)
            high = value.astype(jnp.bfloat16)
            sent[phase, p, pl.ds(0, full // 2)] = high
            sent[phase, p, pl.ds(full // 2, full // 2)] = (value - high.astype(jnp.float32)).astype(jnp.bfloat16)
            if edges:
                sent[phase, p, pl.ds(full, objectives)] = borders[p].astype(jnp.bfloat16)
        if edges:
            for copies, here in far_copies(phase, to_lines):
                @pl.when(here)
                def _():
                    for copy in copies:
                        copy.start()
        rows = rows_of(edges)
        for to in peers():
            remote(
                sent.at[phase, to, rows], got.at[phase, me, rows],
                (send_sem.at[phase], recv_sem.at[phase]), (to, mk),
            ).start()
        got[phase, me, rows] = sent[phase, me, rows]

    def far_copies(phase, to_lines):
        index = phase // 2
        copies = []
        sems = [(far_send.at[phase, d], far_recv.at[phase, d]) for d in range(2)]
        if to_lines:
            copies.append(([remote(sent_far.at[phase, 0], lines_far.at[index, 0, me], sems[0], (0, after_k))], mk + 1 < n_py))
            copies.append(([remote(sent_far.at[phase, 1], lines_far.at[index, 1, me], sems[1], (n_px - 1, before_k))], mk > 0))
        else:
            copies.append((
                [remote(sent_far.at[phase, 0], cells_far.at[index, 0], sems[0], (d, after_k)) for d in range(n_px)],
                (me == n_px - 1) & (mk + 1 < n_py),
            ))
            copies.append((
                [remote(sent_far.at[phase, 1], cells_far.at[index, 1], sems[1], (d, before_k)) for d in range(n_px)],
                (me == 0) & (mk > 0),
            ))
        return copies

    def receive(phase, edges, to_lines):
        await_bytes(got.at[phase, pl.ds(0, n_px - 1), rows_of(edges)], recv_sem.at[phase])
        blocks = []
        for p in range(n_px):
            value = got[phase, p, pl.ds(0, full // 2)].astype(jnp.float32)
            value = value + got[phase, p, pl.ds(full // 2, full // 2)].astype(jnp.float32)
            blocks.append([value[i * objectives : (i + 1) * objectives] for i in range(parts)])
        if to_lines:
            tiles = [t for i in range(parts) for t in exchanged([block[i] for block in blocks], 1)]
        else:
            tiles = exchanged([t for block in blocks for t in block], n_px)
        if not edges:
            return tiles
        borders = [got[phase, p, pl.ds(full, objectives)].astype(jnp.float32) for p in range(n_px)]
        index = phase // 2
        zero = jnp.zeros((objectives, width), jnp.float32)
        up, down = zero, zero
        if to_lines:
            @pl.when((me == 0) & (mk > 0))
            def _():
                await_bytes(lines_far.at[index, 0], far_recv.at[phase, 0])

            @pl.when((me == n_px - 1) & (mk + 1 < n_py))
            def _():
                await_bytes(lines_far.at[index, 1], far_recv.at[phase, 1])

            for p in range(n_px):
                up = jnp.where(digit == p, rolled(borders[p] + lines_far[index, 0, p], p + 1 - n_px), up)
                down = jnp.where(digit == p, rolled(borders[p] + lines_far[index, 1, p], p), down)
            return tiles, up, down, None, None

        @pl.when(mk > 0)
        def _():
            await_bytes(cells_far.at[index, 0], far_recv.at[phase, 0])

        @pl.when(mk + 1 < n_py)
        def _():
            await_bytes(cells_far.at[index, 1], far_recv.at[phase, 1])

        for p in range(n_px):
            up = jnp.where(group == p, rolled(borders[p], (p + 1) * cells_x), up)
            down = jnp.where(group == p, rolled(borders[p], p * cells_x), down)
        left, right = cells_far[index, 0], cells_far[index, 1]
        lefts = [pltpu.roll(left, lax.rem(2 * width - x * n_px - me, width), 1) for x in range(cells_x)]
        rights = [pltpu.roll(right, lax.rem(2 * width - 1 - x * n_px - me, width), 1) for x in range(cells_x)]
        return tiles, up, down, lefts, rights

    def beside(z, t, lefts, rights):
        if lefts is not None:
            left = jnp.where(lane == 0, lefts[t], pltpu.roll(z, 1, 1))
            right = jnp.where(lane == width - 1, rights[t], pltpu.roll(z, width - 1, 1))
            return left, right
        left = jnp.where(ring == 0, jnp.where(lane == 0, 0.0, pltpu.roll(z, n_px + 1, 1)), pltpu.roll(z, n_px, 1))
        right = jnp.where(
            ring == cells_x - 1,
            jnp.where(lane == width - 1, 0.0, pltpu.roll(z, width - n_px - 1, 1)),
            pltpu.roll(z, width - n_px, 1),
        )
        return left, right

    def residual(right_side, field, coefs, tile_next, tile_prev, lane_next, lane_prev):
        tiles, up, down, lefts, rights = field
        result = []
        for t in range(cells_x):
            z = tiles[t]
            before = up if t == 0 else tiles[t - 1]
            after = down if t == last else tiles[t + 1]
            left, right = beside(z, t, lefts, rights)

            def c(row):
                return coefs[t, pl.ds(row, 1), :]

            applied = c(DIAG) * z - c(tile_next) * after - c(tile_prev) * before - c(lane_next) * right - c(lane_prev) * left
            result.append(right_side[t] - applied)
        return result

    def relax(blocks, res):
        result = []
        for t in range(0, cells_x, 2):
            product = lax.dot_general(
                jnp.concatenate(res[t : t + 2], 0).astype(jnp.bfloat16), blocks[pl.ds(t, 2)].reshape(2 * width, width),
                (((1,), (1,)), ((), ())), preferred_element_type=jnp.float32,
            )
            result += [product[:objectives, :width], product[objectives:, width:]]
        return result

    def reorder_blocks():
        shape = (width, width)
        row, column = lax.broadcasted_iota(jnp.int32, shape, 0), lax.broadcasted_iota(jnp.int32, shape, 1)
        place = (column == (row % n_px) * cells_x + row // n_px).astype(jnp.float32).astype(jnp.bfloat16)
        for t in range(cells_x):
            value = lax.dot_general(
                blocks_x[t], place, (((1,), (1,)), ((), ())), preferred_element_type=jnp.float32
            ).astype(jnp.bfloat16)
            blocks_x[t] = jnp.dot(place, value, preferred_element_type=jnp.float32).astype(jnp.bfloat16)

    barrier = pltpu.get_barrier_semaphore()
    for to in peers():
        pl.semaphore_signal(barrier, inc=1, device_id=(to, mk), device_id_type=MESH)
    for d in range(1, n_py):
        pl.semaphore_signal(barrier, inc=1, device_id=(me, lax.rem(mk + d, n_py)), device_id_type=MESH)

    pairs = (
        (weight, records.at[mk, pl.ds(0, objectives)]), (tile, tile_here), (cell, cell_here), (owner, owner_here),
        (coef, coef_here), (grad, grad_here), (inv_x, blocks_x),
    )
    fetches = [pltpu.make_async_copy(*pair, load_sem.at[i]) for i, pair in enumerate(pairs)]
    for fetch in fetches:
        fetch.start()
    own_blocks = pltpu.make_async_copy(inv_y.at[:, mk], blocks_y.at[pl.ds(mk * per_y, per_y)], inv_own)
    own_blocks.start()
    lines_far[...] = jnp.zeros_like(lines_far)
    cells_far[...] = jnp.zeros_like(cells_far)

    def record_copy(d):
        return remote(records.at[mk], records.at[mk], (rec_send, rec_recv), (me, lax.rem(mk + d, n_py)))

    def block_copy(d):
        to = lax.rem(mk + d, n_py)
        return remote(
            inv_y.at[:, to], blocks_y.at[pl.ds(mk * per_y, per_y)], (inv_send, inv_recv), (me, to)
        )

    copy_x = remote(coef_here.at[1], near_x, (near_send.at[0], near_recv.at[0]), (lax.rem(me + 1, n_px), mk))
    copy_y = remote(coef_here.at[2], near_y, (near_send.at[1], near_recv.at[1]), (me, after_k))
    has_x, has_y = me + 1 < n_px, mk + 1 < n_py

    count = weight.shape[1]
    span = cells_x * objectives
    x_number = lax.broadcasted_iota(jnp.int32, (cells_x, objectives, count), 0).astype(jnp.float32)
    y_number = lax.broadcasted_iota(jnp.int32, (width, count), 0).astype(jnp.float32)

    def loads_from(source, s):
        cells = records[source, pl.ds(objectives + 2, 1)]
        owners = records[source, pl.ds(objectives + 3, 1)]
        at_x = jnp.floor(cells * (1.0 / width))
        at_y = cells - at_x * width
        at_x = jnp.where(owners == mk.astype(jnp.float32), at_x, -1.0)
        hit = x_number == at_x[None]
        spread = (y_number == at_y).astype(jnp.float32).astype(jnp.bfloat16)
        value = records[source, pl.ds(objectives + s, 1)] * records[source, pl.ds(0, objectives)]
        high = value.astype(jnp.bfloat16).astype(jnp.float32)
        rows = [
            jnp.where(hit, piece[None], 0.0).reshape(span, count).astype(jnp.bfloat16)
            for piece in (high, value - high)
        ]
        total = lax.dot_general(
            jnp.concatenate(rows, 0), spread, (((1,), (1,)), ((), ())), preferred_element_type=jnp.float32
        )
        return total[:span] + total[span:]

    for fetch in fetches[:4]:
        fetch.wait()
    records[mk, pl.ds(objectives, 2)] = tile_here[...]
    records[mk, pl.ds(objectives + 2, 1)] = cell_here[...].astype(jnp.float32)
    records[mk, pl.ds(objectives + 3, 1)] = owner_here[...].astype(jnp.float32)
    fetches[4].wait()
    for s in range(2):
        loads[s] = loads_from(mk, s)
    pl.semaphore_wait(barrier, n_px + n_py - 2)
    for d in range(1, n_py):
        record_copy(d).start()
    pl.when(has_x)(lambda: copy_x.start())
    pl.when(has_y)(lambda: copy_y.start())
    fetches[5].wait()
    fetches[6].wait()
    reorder_blocks()
    await_bytes(records.at[pl.ds(0, n_py - 1)], rec_recv)

    def add_loads(s):
        total = loads[s]
        for d in range(1, n_py):
            total = total + loads_from(lax.rem(mk + d, n_py), s)
        loads[s] = total

    add_loads(1)

    def loaded(s):
        return [
            grad_here[s, :, t, :] + loads[s, pl.ds(t * objectives, objectives), :]
            for t in range(cells_x)
        ]

    def solve(base, right_side):
        send(base + B_TO_LINES, right_side, False, True)
        if base == 0:
            for step in range(1, n_py):
                block_copy(step).start()
            share_coefficients()
            add_loads(0)
        line_side = receive(base + B_TO_LINES, False, True)
        send(base + Z1_TO_CELLS, relax(blocks_x, line_side), True, False)
        field = receive(base + Z1_TO_CELLS, True, False)
        res = residual(right_side, field, coef_cells, COND_X, LOW_X, COND_Y, LOW_Y)
        if base == 0:
            await_bytes(blocks_y.at[pl.ds(0, per_y * (n_py - 1))], inv_recv)
            own_blocks.wait()
        update = relax(blocks_y, res)
        send(base + Z2_TO_LINES, [z + u for z, u in zip(field[0], update)], True, True)
        field = receive(base + Z2_TO_LINES, True, True)
        if base == 0:
            for t, value in enumerate(receive(COEF, False, True)):
                coef_lines[t] = value
        update = relax(blocks_x, residual(line_side, field, coef_lines, COND_Y, LOW_Y, COND_X, LOW_X))
        send(base + Z3_TO_CELLS, [z + u for z, u in zip(field[0], update)], True, False)
        field = receive(base + Z3_TO_CELLS, True, False)
        update = relax(blocks_y, residual(right_side, field, coef_cells, COND_X, LOW_X, COND_Y, LOW_Y))
        return [z + u for z, u in zip(field[0], update)]

    def share_coefficients():
        storage, conduct_x, conduct_y = coef_here[0], coef_here[1], coef_here[2]
        pl.when(me > 0)(lambda: await_bytes(near_x, near_recv.at[0]))
        pl.when(mk > 0)(lambda: await_bytes(near_y, near_recv.at[1]))
        row = lax.broadcasted_iota(jnp.int32, conduct_x.shape, 0)
        column = lax.broadcasted_iota(jnp.int32, conduct_x.shape, 1)
        below_x = jnp.where(me > 0, pltpu.roll(near_x[...], 1, 0), 0.0)
        below_y = jnp.where(mk > 0, pltpu.roll(near_y[...], 1, 1), 0.0)
        lower_x = jnp.where(row == 0, below_x, pltpu.roll(conduct_x, 1, 0))
        lower_y = jnp.where(column == 0, below_y, pltpu.roll(conduct_y, 1, 1))
        diagonal = storage + conduct_x + lower_x + conduct_y + lower_y
        tiles = []
        for t in range(cells_x):
            value = jnp.zeros((objectives, width), jnp.float32)
            for number, array in enumerate((diagonal, conduct_x, lower_x, conduct_y, lower_y, storage)):
                value = jnp.where(sub == number, array[t : t + 1], value)
            coef_cells[t] = value
            tiles.append(value)
        send(COEF, tiles, False, True)

    def keep(s, tiles):
        for t in range(cells_x):
            out[s, :, t, :] = tiles[t]

    second = solve(0, loaded(1))
    keep(1, second)
    first_side = [b + coef_cells[t, pl.ds(STORE, 1), :] * second[t] for t, b in enumerate(loaded(0))]
    keep(0, solve(4, first_side))

    for phase in range(9):
        edges = phase != COEF and phase % 4 != B_TO_LINES
        await_bytes(sent.at[phase, pl.ds(0, n_px - 1), rows_of(edges)], send_sem.at[phase])
        if edges:
            for copies, here in far_copies(phase, phase % 4 == Z2_TO_LINES):
                @pl.when(here)
                def _():
                    for copy in copies:
                        copy.wait_send()
    await_bytes(records.at[pl.ds(0, n_py - 1)], rec_send)
    await_bytes(blocks_y.at[pl.ds(0, per_y * (n_py - 1))], inv_send)
    pl.when(has_x)(lambda: copy_x.wait_send())
    pl.when(has_y)(lambda: copy_y.wait_send())


def fused_shards(
    objective_grad, coefficients, inv_x, inv_y, perf_cell, perf_owner, perf_tile, perf_weight
):
    steps, objectives, cells_x, width = objective_grad.shape
    n_px, n_py = lax.axis_size("px"), lax.axis_size("py")
    segment = inv_x.shape[3]
    records = perf_cell.shape[0]
    parts = cells_x // n_px
    f32 = jnp.float32
    dma = pltpu.SemaphoreType.DMA
    vmem = pl.BlockSpec(memory_space=pltpu.VMEM)
    anywhere = pl.BlockSpec(memory_space=pl.ANY)
    tile = (objectives, width)
    result = pl.pallas_call(
        functools.partial(fused, n_px, n_py, cells_x),
        out_shape=pltpu.VMEM(objective_grad.shape, f32),
        in_specs=[anywhere] * 8,
        out_specs=vmem,
        scratch_shapes=[
            pltpu.VMEM((9, n_px, 3 * parts * objectives, width), jnp.bfloat16),
            pltpu.VMEM((9, n_px, 3 * parts * objectives, width), jnp.bfloat16),
            pltpu.VMEM((8, 2) + tile, f32),
            pltpu.VMEM((4, 2, n_px) + tile, f32),
            pltpu.VMEM((4, 2) + tile, f32),
            pltpu.VMEM((n_py, 2 * objectives, records), f32),
            pltpu.VMEM((cells_x, width), f32),
            pltpu.VMEM((cells_x, width), f32),
            pltpu.VMEM((cells_x,) + tile, f32),
            pltpu.VMEM((cells_x,) + tile, f32),
            pltpu.VMEM((cells_x, segment, segment), jnp.bfloat16),
            pltpu.VMEM((steps, objectives * cells_x, width), f32),
            pltpu.VMEM(objective_grad.shape, f32),
            pltpu.VMEM(coefficients.shape, f32),
            pltpu.VMEM((cells_x, segment, segment), jnp.bfloat16),
            pltpu.VMEM((1, records), jnp.int32),
            pltpu.VMEM((1, records), jnp.int32),
            pltpu.VMEM((2, records), f32),
            dma((9,)), dma((9,)), dma((8, 2)), dma((8, 2)),
            dma, dma, dma((2,)), dma((2,)), dma, dma, dma, dma((7,)),
        ],
        compiler_params=pltpu.CompilerParams(collective_id=0, has_side_effects=True),
    )(
        objective_grad,
        coefficients,
        inv_x.reshape(inv_x.shape[0], segment, segment),
        inv_y.reshape(inv_y.shape[1:]),
        perf_cell.reshape(1, records),
        perf_owner.reshape(1, records),
        perf_tile,
        perf_weight,
    )
    return result


def per_device(*args):
    grad, inv_x = args[0], args[2]
    objectives, cells_x, width = grad.shape[1:]
    n_px = lax.axis_size("px")
    fits = (
        inv_x.shape[2] == 1
        and width == inv_x.shape[3] == 128
        and cells_x * n_px == width
        and inv_x.shape[0] == cells_x
        and cells_x == 2 * n_px
        and n_px == objectives == 8
    )
    return fused_shards(*args) if fits else shards(*args)


def solution(mesh):
    return jax.shard_map(
        per_device,
        mesh=mesh,
        in_specs=(
            P(None, None, "px", "py"),
            P(None, "px", "py"),
            P("px", "py", None, None, None),
            P("px", "py", None, None, None),
            P(("px", "py")),
            P(("px", "py"), None),
            P(None, ("px", "py")),
            P(None, ("px", "py")),
        ),
        out_specs=P(None, None, "px", "py"),
        check_vma=False,
    )
```

```python
import functools

import jax
import jax.numpy as jnp
from jax import lax
from jax.experimental import pallas as pl
from jax.experimental.pallas import tpu as pltpu
from jax.sharding import PartitionSpec as P


def passed_along(value, axis, steps):
    count = lax.axis_size(axis)
    leading, last = (max(0, -steps), min(count, count - steps))
    return lax.ppermute(value, axis, [(source, source + steps) for source in range(leading, last)])


def extended(cells, sides, width):
    for axis, dim in sides:
        count = lax.axis_size(axis)
        ends = count - 1
        head = lax.slice_in_dim(cells, 0, width, axis=dim)
        tail = lax.slice_in_dim(cells, cells.shape[dim] - width, cells.shape[dim], axis=dim)
        cells = jnp.concatenate(
            [
                lax.ppermute(tail, axis, [(i, (i + 1) % count) for i in range(ends)]),
                cells,
                lax.ppermute(head, axis, [((i + 1) % count, i) for i in range(ends)]),
            ],
            axis=dim,
        )
    return cells


def shards(
    objective_grad, coefficients, inv_x, inv_y, perf_cell, perf_owner, perf_tile, perf_weight
):
    objectives = objective_grad.shape[1]
    width_x = coefficients.shape[1]
    width_y = coefficients.shape[2]
    storage = coefficients[0]
    conduct_x = coefficients[1]
    conduct_y = coefficients[2]
    below_x = passed_along(conduct_x[-1:, :], "px", 1)
    below_y = passed_along(conduct_y[:, -1:], "py", 1)
    lower_x = jnp.concatenate([below_x, conduct_x[:-1, :]], 0)
    lower_y = jnp.concatenate([below_y, conduct_y[:, :-1]], 1)
    diagonal = storage + conduct_x + lower_x + conduct_y + lower_y
    segment = inv_x.shape[3]
    blocks_x = inv_x.reshape(inv_x.shape[0], inv_x.shape[2], segment, segment)
    blocks_y = inv_y.reshape(inv_y.shape[1], inv_y.shape[2], segment, segment)

    def operate(iterate):
        padded = extended(iterate, (("px", 1), ("py", 2)), 1)
        return (
            diagonal * iterate
            - conduct_x * padded[:, 2:, 1:-1]
            - lower_x * padded[:, :-2, 1:-1]
            - conduct_y * padded[:, 1:-1, 2:]
            - lower_y * padded[:, 1:-1, :-2]
        )

    def relax_first(residual):
        turned = jnp.swapaxes(residual.astype(jnp.bfloat16), 1, 2)
        line_rows = lax.all_to_all(turned, "px", split_axis=1, concat_axis=2, tiled=True)
        shaped = line_rows.reshape(objectives, line_rows.shape[1], -1, segment)
        update = jnp.einsum("rkij,qrkj->qrki", blocks_x, shaped, preferred_element_type=jnp.float32)
        returned = lax.all_to_all(
            update.reshape(line_rows.shape), "px", split_axis=2, concat_axis=1, tiled=True
        )
        return jnp.swapaxes(returned, 1, 2)

    def relax_second(residual):
        line_rows = lax.all_to_all(
            residual.astype(jnp.bfloat16), "py", split_axis=1, concat_axis=2, tiled=True
        )
        shaped = line_rows.reshape(objectives, line_rows.shape[1], -1, segment)
        update = jnp.einsum("xkij,qxkj->qxki", blocks_y, shaped, preferred_element_type=jnp.float32)
        return lax.all_to_all(
            update.reshape(line_rows.shape), "py", split_axis=2, concat_axis=1, tiled=True
        )

    def relaxed_solve(right_side):
        iterate = relax_first(right_side)
        iterate = iterate + relax_second(right_side - operate(iterate))
        iterate = iterate + relax_first(right_side - operate(iterate))
        iterate = iterate + relax_second(right_side - operate(iterate))
        return iterate

    records = perf_cell.shape[0]
    owners = lax.axis_size("py")
    capacity = 2 * records // owners
    payload = jnp.concatenate([perf_tile, perf_weight, perf_cell.astype(jnp.float32)[None, :]], 0)
    owner_index = perf_owner[:, 0]
    onehot = (owner_index[:, None] == jnp.arange(owners, dtype=jnp.int32)[None, :]).astype(
        jnp.int32
    )
    rank_in_owner = jnp.sum((jnp.cumsum(onehot, 0) - 1) * onehot, axis=1)
    slot_index = owner_index * capacity + rank_in_owner
    packed = (
        jnp.zeros((payload.shape[0], owners * capacity), jnp.float32).at[:, slot_index].set(payload)
    )
    arrived = lax.all_to_all(packed, "py", split_axis=1, concat_axis=1, tiled=True)
    tile_rows = arrived[0:2]
    weight_rows = arrived[2 : 2 + objectives]
    cell_index = arrived[2 + objectives].astype(jnp.int32)
    values = tile_rows[:, None, :] * weight_rows[None, :, :]
    well_loads = (
        jnp.zeros((2, objectives, width_x * width_y), jnp.float32).at[:, :, cell_index].add(values)
    )
    well_loads = well_loads.reshape(2, objectives, width_x, width_y)
    second_adjoint = relaxed_solve(objective_grad[1] + well_loads[1])
    first_adjoint = relaxed_solve(objective_grad[0] + well_loads[0] + storage * second_adjoint)
    return jnp.stack([first_adjoint, second_adjoint])


MESH = pl.DeviceIdType.MESH
DIAG, COND_X, LOW_X, COND_Y, LOW_Y, STORE = range(6)
B_TO_LINES, Z1_TO_CELLS, Z2_TO_LINES, Z3_TO_CELLS = range(4)
COEF = 8


def skewed_swap(tiles, step, lane):
    count, width = len(tiles), lane.shape[1]
    digit = (lane // step) % count
    moved = [t if i == 0 else pltpu.roll(t, i * step % width, 1) for i, t in enumerate(tiles)]
    out = [moved[-i % count] for i in range(count)]
    bit = 1
    while bit < count:
        on = (digit & bit) != 0
        out = [jnp.where(on, out[(i - bit) % count], out[i]) for i in range(count)]
        bit *= 2
    return out


def fused(
    n_px, n_py, cells_x,
    grad, coef, inv_x, inv_y, cell, owner, tile, weight,
    out,
    sent, got, sent_far, lines_far, cells_far, records, near_x, near_y, coef_cells, coef_lines, blocks_y, loads,
    grad_here, coef_here, blocks_x, cell_here, owner_here, tile_here,
    send_sem, recv_sem, far_send, far_recv, rec_send, rec_recv, near_send, near_recv, inv_send, inv_recv, inv_own, load_sem,
):
    me = lax.axis_index("px")
    mk = lax.axis_index("py")
    after_k, before_k = lax.rem(mk + 1, n_py), lax.rem(mk + n_py - 1, n_py)
    objectives, width = weight.shape[0], coef.shape[2]
    parts = cells_x // n_px
    last = cells_x - 1
    per_y = inv_y.shape[0]
    lane = lax.broadcasted_iota(jnp.int32, (objectives, width), 1)
    group = lane // cells_x
    digit = lane % n_px
    ring = lane // n_px
    sub = lax.broadcasted_iota(jnp.int32, (objectives, width), 0)

    def remote(source, target, sems, where):
        return pltpu.make_async_remote_copy(
            src_ref=source, dst_ref=target, send_sem=sems[0], recv_sem=sems[1],
            device_id=where, device_id_type=MESH,
        )

    def await_bytes(ref, sem):
        pltpu.make_async_copy(ref, ref, sem).wait()

    def rolled(value, amount):
        return value if amount % width == 0 else pltpu.roll(value, amount % width, 1)

    def exchanged(tiles, step):
        return [rolled(t, -i * step) for i, t in enumerate(skewed_swap(tiles, step, lane))]

    def peers():
        low = me < n_px // 2
        for i in range(n_px - 1):
            down, up = n_px - 1 - i, i
            down = jnp.where(down <= me, down - 1, down)
            up = jnp.where(up >= me, up + 1, up)
            yield jnp.where(low, down, up)

    full = 2 * parts * objectives

    def rows_of(edges):
        return pl.ds(0, full + objectives if edges else full)

    def send_far(phase, after, before, to_lines):
        sent_far[phase, 0] = after.astype(jnp.bfloat16)
        sent_far[phase, 1] = before.astype(jnp.bfloat16)
        for copies, here in far_copies(phase, to_lines):
            @pl.when(here)
            def _():
                for copy in copies:
                    copy.start()

    def send(phase, tiles, edges, to_lines):
        zero = jnp.zeros((objectives, width), jnp.float32)
        borders = None
        if to_lines:
            turned = exchanged(tiles, n_px)
            packed = [[turned[parts * p + i] for i in range(parts)] for p in range(n_px)]
            if edges:
                send_far(phase, turned[last], turned[0], to_lines)
                borders = [
                    jnp.where(
                        digit == n_px - 1,
                        zero if p == 0 else packed[p - 1][parts - 1],
                        zero if p == n_px - 1 else packed[p + 1][0],
                    )
                    for p in range(n_px)
                ]
        else:
            send_far(phase, tiles[last], tiles[0], to_lines)
            halves = [skewed_swap(tiles[i * n_px : (i + 1) * n_px], 1, lane) for i in range(parts)]
            packed = [[rolled(halves[i][p], -p) for i in range(parts)] for p in range(n_px)]
            borders = []
            for p in range(n_px):
                value = zero
                if p > 0:
                    high = jnp.where(
                        ring == cells_x - 1, packed[p - 1][1], rolled(halves[0][p - 1], -(p - 1) - n_px)
                    )
                    value = jnp.where(ring >= cells_x - 2, high, value)
                if p < n_px - 1:
                    low = jnp.where(ring == 0, packed[p + 1][0], rolled(halves[1][p + 1], n_px - (p + 1)))
                    value = jnp.where(ring <= 1, low, value)
                borders.append(value)
        for p in range(n_px):
            value = jnp.concatenate(packed[p], 0)
            high = value.astype(jnp.bfloat16)
            sent[phase, p, pl.ds(0, full // 2)] = high
            sent[phase, p, pl.ds(full // 2, full // 2)] = (value - high.astype(jnp.float32)).astype(jnp.bfloat16)
            if edges:
                sent[phase, p, pl.ds(full, objectives)] = borders[p].astype(jnp.bfloat16)
        rows = rows_of(edges)
        for to in peers():
            remote(
                sent.at[phase, to, rows], got.at[phase, me, rows],
                (send_sem.at[phase], recv_sem.at[phase]), (to, mk),
            ).start()
        got[phase, me, rows] = sent[phase, me, rows]

    def far_copies(phase, to_lines):
        index = phase // 2
        copies = []
        sems = [(far_send.at[phase, d], far_recv.at[phase, d]) for d in range(2)]
        if to_lines:
            copies.append(([remote(sent_far.at[phase, 0], lines_far.at[index, 0, me], sems[0], (0, after_k))], mk + 1 < n_py))
            copies.append(([remote(sent_far.at[phase, 1], lines_far.at[index, 1, me], sems[1], (n_px - 1, before_k))], mk > 0))
        else:
            copies.append((
                [remote(sent_far.at[phase, 0], cells_far.at[index, 0], sems[0], (d, after_k)) for d in range(n_px)],
                (me == n_px - 1) & (mk + 1 < n_py),
            ))
            copies.append((
                [remote(sent_far.at[phase, 1], cells_far.at[index, 1], sems[1], (d, before_k)) for d in reversed(range(n_px))],
                (me == 0) & (mk > 0),
            ))
        return copies

    def receive(phase, edges, to_lines):
        index = phase // 2
        await_bytes(got.at[phase, pl.ds(0, n_px - 1), rows_of(edges)], recv_sem.at[phase])
        if edges:
            for d, there in enumerate((mk > 0, mk + 1 < n_py)):
                far = lines_far.at[index, d] if to_lines else cells_far.at[index, d]
                here = there & (me == (0, n_px - 1)[d]) if to_lines else there

                @pl.when(here)
                def _():
                    await_bytes(far, far_recv.at[phase, d])
        blocks = []
        for p in range(n_px):
            value = got[phase, p, pl.ds(0, full // 2)].astype(jnp.float32)
            value = value + got[phase, p, pl.ds(full // 2, full // 2)].astype(jnp.float32)
            blocks.append([value[i * objectives : (i + 1) * objectives] for i in range(parts)])
        if to_lines:
            tiles = [t for i in range(parts) for t in exchanged([block[i] for block in blocks], 1)]
        else:
            tiles = exchanged([t for block in blocks for t in block], n_px)
        if not edges:
            return tiles
        borders = [got[phase, p, pl.ds(full, objectives)].astype(jnp.float32) for p in range(n_px)]
        zero = jnp.zeros((objectives, width), jnp.float32)
        up, down = zero, zero
        if to_lines:
            for p in range(n_px):
                up = jnp.where(digit == p, rolled(borders[p] + lines_far[index, 0, p].astype(jnp.float32), p + 1 - n_px), up)
                down = jnp.where(digit == p, rolled(borders[p] + lines_far[index, 1, p].astype(jnp.float32), p), down)
            return tiles, up, down, None, None

        for p in range(n_px):
            up = jnp.where(group == p, rolled(borders[p], (p + 1) * cells_x), up)
            down = jnp.where(group == p, rolled(borders[p], p * cells_x), down)
        left, right = [cells_far[index, d].astype(jnp.float32) for d in range(2)]
        lefts = [pltpu.roll(left, lax.rem(2 * width - x * n_px - me, width), 1) for x in range(cells_x)]
        rights = [pltpu.roll(right, lax.rem(2 * width - 1 - x * n_px - me, width), 1) for x in range(cells_x)]
        return tiles, up, down, lefts, rights

    def beside(z, t, lefts, rights):
        if lefts is not None:
            left = jnp.where(lane == 0, lefts[t], pltpu.roll(z, 1, 1))
            right = jnp.where(lane == width - 1, rights[t], pltpu.roll(z, width - 1, 1))
            return left, right
        left = jnp.where(ring == 0, jnp.where(lane == 0, 0.0, pltpu.roll(z, n_px + 1, 1)), pltpu.roll(z, n_px, 1))
        right = jnp.where(
            ring == cells_x - 1,
            jnp.where(lane == width - 1, 0.0, pltpu.roll(z, width - n_px - 1, 1)),
            pltpu.roll(z, width - n_px, 1),
        )
        return left, right

    def residual(right_side, field, coefs, tile_next, tile_prev, lane_next, lane_prev):
        tiles, up, down, lefts, rights = field
        result = []
        for t in range(cells_x):
            z = tiles[t]
            before = up if t == 0 else tiles[t - 1]
            after = down if t == last else tiles[t + 1]
            left, right = beside(z, t, lefts, rights)

            def c(row):
                return coefs[t, pl.ds(row, 1), :]

            applied = c(DIAG) * z - c(tile_next) * after - c(tile_prev) * before - c(lane_next) * right - c(lane_prev) * left
            result.append(right_side[t] - applied)
        return result

    def relax(blocks, res):
        result = []
        for t in range(0, cells_x, 2):
            product = lax.dot_general(
                jnp.concatenate(res[t : t + 2], 0).astype(jnp.bfloat16), blocks[pl.ds(t, 2)].reshape(2 * width, width),
                (((1,), (1,)), ((), ())), preferred_element_type=jnp.float32,
            )
            result += [product[:objectives, :width], product[objectives:, width:]]
        return result

    def reorder_blocks():
        shape = (width, width)
        row, column = lax.broadcasted_iota(jnp.int32, shape, 0), lax.broadcasted_iota(jnp.int32, shape, 1)
        place = (column == (row % n_px) * cells_x + row // n_px).astype(jnp.float32).astype(jnp.bfloat16)
        for t in range(cells_x):
            value = lax.dot_general(
                blocks_x[t], place, (((1,), (1,)), ((), ())), preferred_element_type=jnp.float32
            ).astype(jnp.bfloat16)
            blocks_x[t] = jnp.dot(place, value, preferred_element_type=jnp.float32).astype(jnp.bfloat16)

    barrier = pltpu.get_barrier_semaphore()
    for to in peers():
        pl.semaphore_signal(barrier, inc=1, device_id=(to, mk), device_id_type=MESH)
    for d in range(1, n_py):
        pl.semaphore_signal(barrier, inc=1, device_id=(me, lax.rem(mk + d, n_py)), device_id_type=MESH)

    pairs = (
        (weight, records.at[mk, pl.ds(0, objectives)]), (tile, tile_here), (cell, cell_here), (owner, owner_here),
        (coef, coef_here), (grad, grad_here), (inv_x, blocks_x),
    )
    fetches = [pltpu.make_async_copy(*pair, load_sem.at[i]) for i, pair in enumerate(pairs)]
    for fetch in fetches:
        fetch.start()
    own_blocks = pltpu.make_async_copy(inv_y.at[:, mk], blocks_y.at[pl.ds(mk * per_y, per_y)], inv_own)
    own_blocks.start()
    lines_far[...] = jnp.zeros_like(lines_far)
    cells_far[...] = jnp.zeros_like(cells_far)

    def record_copy(d):
        return remote(records.at[mk], records.at[mk], (rec_send, rec_recv), (me, lax.rem(mk + d, n_py)))

    def block_copy(d):
        to = lax.rem(mk + d, n_py)
        return remote(
            inv_y.at[:, to], blocks_y.at[pl.ds(mk * per_y, per_y)], (inv_send, inv_recv), (me, to)
        )

    copy_x = remote(coef_here.at[1], near_x, (near_send.at[0], near_recv.at[0]), (lax.rem(me + 1, n_px), mk))
    copy_y = remote(coef_here.at[2], near_y, (near_send.at[1], near_recv.at[1]), (me, after_k))
    has_x, has_y = me + 1 < n_px, mk + 1 < n_py

    count = weight.shape[1]
    span = cells_x * objectives
    x_number = lax.broadcasted_iota(jnp.int32, (cells_x, objectives, count), 0).astype(jnp.float32)
    y_number = lax.broadcasted_iota(jnp.int32, (width, count), 0).astype(jnp.float32)

    def loads_from(source, s):
        cells = records[source, pl.ds(objectives + 2, 1)]
        owners = records[source, pl.ds(objectives + 3, 1)]
        at_x = jnp.floor(cells * (1.0 / width))
        at_y = cells - at_x * width
        at_x = jnp.where(owners == mk.astype(jnp.float32), at_x, -1.0)
        hit = x_number == at_x[None]
        spread = (y_number == at_y).astype(jnp.float32).astype(jnp.bfloat16)
        value = records[source, pl.ds(objectives + s, 1)] * records[source, pl.ds(0, objectives)]
        high = value.astype(jnp.bfloat16).astype(jnp.float32)
        rows = [
            jnp.where(hit, piece[None], 0.0).reshape(span, count).astype(jnp.bfloat16)
            for piece in (high, value - high)
        ]
        total = lax.dot_general(
            jnp.concatenate(rows, 0), spread, (((1,), (1,)), ((), ())), preferred_element_type=jnp.float32
        )
        return total[:span] + total[span:]

    for fetch in fetches[:4]:
        fetch.wait()
    records[mk, pl.ds(objectives, 2)] = tile_here[...]
    records[mk, pl.ds(objectives + 2, 1)] = cell_here[...].astype(jnp.float32)
    records[mk, pl.ds(objectives + 3, 1)] = owner_here[...].astype(jnp.float32)
    fetches[4].wait()
    for s in range(2):
        loads[s] = loads_from(mk, s)
    pl.semaphore_wait(barrier, n_px + n_py - 2)
    for d in range(1, n_py):
        record_copy(d).start()
    pl.when(has_x)(lambda: copy_x.start())
    pl.when(has_y)(lambda: copy_y.start())
    fetches[5].wait()
    fetches[6].wait()
    reorder_blocks()
    await_bytes(records.at[pl.ds(0, n_py - 1)], rec_recv)

    def add_loads(s):
        total = loads[s]
        for d in range(1, n_py):
            total = total + loads_from(lax.rem(mk + d, n_py), s)
        loads[s] = total

    add_loads(1)

    def loaded(s):
        return [
            grad_here[s, :, t, :] + loads[s, pl.ds(t * objectives, objectives), :]
            for t in range(cells_x)
        ]

    def solve(base, right_side):
        send(base + B_TO_LINES, right_side, False, True)
        if base == 0:
            for step in range(1, n_py):
                block_copy(step).start()
            share_coefficients()
            add_loads(0)
        line_side = receive(base + B_TO_LINES, False, True)
        send(base + Z1_TO_CELLS, relax(blocks_x, line_side), True, False)
        if base == 0:
            for t, value in enumerate(receive(COEF, False, True)):
                coef_lines[t] = value
            await_bytes(blocks_y.at[pl.ds(0, per_y * (n_py - 1))], inv_recv)
            own_blocks.wait()
        field = receive(base + Z1_TO_CELLS, True, False)
        res = residual(right_side, field, coef_cells, COND_X, LOW_X, COND_Y, LOW_Y)
        update = relax(blocks_y, res)
        send(base + Z2_TO_LINES, [z + u for z, u in zip(field[0], update)], True, True)
        field = receive(base + Z2_TO_LINES, True, True)
        update = relax(blocks_x, residual(line_side, field, coef_lines, COND_Y, LOW_Y, COND_X, LOW_X))
        send(base + Z3_TO_CELLS, [z + u for z, u in zip(field[0], update)], True, False)
        field = receive(base + Z3_TO_CELLS, True, False)
        update = relax(blocks_y, residual(right_side, field, coef_cells, COND_X, LOW_X, COND_Y, LOW_Y))
        return [z + u for z, u in zip(field[0], update)]

    def share_coefficients():
        storage, conduct_x, conduct_y = coef_here[0], coef_here[1], coef_here[2]
        pl.when(me > 0)(lambda: await_bytes(near_x, near_recv.at[0]))
        pl.when(mk > 0)(lambda: await_bytes(near_y, near_recv.at[1]))
        row = lax.broadcasted_iota(jnp.int32, conduct_x.shape, 0)
        column = lax.broadcasted_iota(jnp.int32, conduct_x.shape, 1)
        below_x = jnp.where(me > 0, pltpu.roll(near_x[...], 1, 0), 0.0)
        below_y = jnp.where(mk > 0, pltpu.roll(near_y[...], 1, 1), 0.0)
        lower_x = jnp.where(row == 0, below_x, pltpu.roll(conduct_x, 1, 0))
        lower_y = jnp.where(column == 0, below_y, pltpu.roll(conduct_y, 1, 1))
        diagonal = storage + conduct_x + lower_x + conduct_y + lower_y
        tiles = []
        for t in range(cells_x):
            value = jnp.zeros((objectives, width), jnp.float32)
            for number, array in enumerate((diagonal, conduct_x, lower_x, conduct_y, lower_y, storage)):
                value = jnp.where(sub == number, array[t : t + 1], value)
            coef_cells[t] = value
            tiles.append(value)
        send(COEF, tiles, False, True)

    def keep(s, tiles):
        for t in range(cells_x):
            out[s, :, t, :] = tiles[t]

    second = solve(0, loaded(1))
    keep(1, second)
    first_side = [b + coef_cells[t, pl.ds(STORE, 1), :] * second[t] for t, b in enumerate(loaded(0))]
    keep(0, solve(4, first_side))

    for phase in range(9):
        edges = phase != COEF and phase % 4 != B_TO_LINES
        await_bytes(sent.at[phase, pl.ds(0, n_px - 1), rows_of(edges)], send_sem.at[phase])
        if edges:
            for copies, here in far_copies(phase, phase % 4 == Z2_TO_LINES):
                @pl.when(here)
                def _():
                    for copy in copies:
                        copy.wait_send()
    await_bytes(records.at[pl.ds(0, n_py - 1)], rec_send)
    await_bytes(blocks_y.at[pl.ds(0, per_y * (n_py - 1))], inv_send)
    pl.when(has_x)(lambda: copy_x.wait_send())
    pl.when(has_y)(lambda: copy_y.wait_send())


def fused_shards(
    objective_grad, coefficients, inv_x, inv_y, perf_cell, perf_owner, perf_tile, perf_weight
):
    steps, objectives, cells_x, width = objective_grad.shape
    n_px, n_py = lax.axis_size("px"), lax.axis_size("py")
    segment = inv_x.shape[3]
    records = perf_cell.shape[0]
    parts = cells_x // n_px
    f32 = jnp.float32
    dma = pltpu.SemaphoreType.DMA
    vmem = pl.BlockSpec(memory_space=pltpu.VMEM)
    anywhere = pl.BlockSpec(memory_space=pl.ANY)
    tile = (objectives, width)
    result = pl.pallas_call(
        functools.partial(fused, n_px, n_py, cells_x),
        out_shape=pltpu.VMEM(objective_grad.shape, f32),
        in_specs=[anywhere] * 8,
        out_specs=vmem,
        scratch_shapes=[
            pltpu.VMEM((9, n_px, 3 * parts * objectives, width), jnp.bfloat16),
            pltpu.VMEM((9, n_px, 3 * parts * objectives, width), jnp.bfloat16),
            pltpu.VMEM((8, 2) + tile, jnp.bfloat16),
            pltpu.VMEM((4, 2, n_px) + tile, jnp.bfloat16),
            pltpu.VMEM((4, 2) + tile, jnp.bfloat16),
            pltpu.VMEM((n_py, 2 * objectives, records), f32),
            pltpu.VMEM((cells_x, width), f32),
            pltpu.VMEM((cells_x, width), f32),
            pltpu.VMEM((cells_x,) + tile, f32),
            pltpu.VMEM((cells_x,) + tile, f32),
            pltpu.VMEM((cells_x, segment, segment), jnp.bfloat16),
            pltpu.VMEM((steps, objectives * cells_x, width), f32),
            pltpu.VMEM(objective_grad.shape, f32),
            pltpu.VMEM(coefficients.shape, f32),
            pltpu.VMEM((cells_x, segment, segment), jnp.bfloat16),
            pltpu.VMEM((1, records), jnp.int32),
            pltpu.VMEM((1, records), jnp.int32),
            pltpu.VMEM((2, records), f32),
            dma((9,)), dma((9,)), dma((8, 2)), dma((8, 2)),
            dma, dma, dma((2,)), dma((2,)), dma, dma, dma, dma((7,)),
        ],
        compiler_params=pltpu.CompilerParams(collective_id=0, has_side_effects=True),
    )(
        objective_grad,
        coefficients,
        inv_x.reshape(inv_x.shape[0], segment, segment),
        inv_y.reshape(inv_y.shape[1:]),
        perf_cell.reshape(1, records),
        perf_owner.reshape(1, records),
        perf_tile,
        perf_weight,
    )
    return result


def per_device(*args):
    grad, inv_x = args[0], args[2]
    objectives, cells_x, width = grad.shape[1:]
    n_px = lax.axis_size("px")
    fits = (
        inv_x.shape[2] == 1
        and width == inv_x.shape[3] == 128
        and cells_x * n_px == width
        and inv_x.shape[0] == cells_x
        and cells_x == 2 * n_px
        and n_px == objectives == 8
    )
    return fused_shards(*args) if fits else shards(*args)


def solution(mesh):
    return jax.shard_map(
        per_device,
        mesh=mesh,
        in_specs=(
            P(None, None, "px", "py"),
            P(None, "px", "py"),
            P("px", "py", None, None, None),
            P("px", "py", None, None, None),
            P(("px", "py")),
            P(("px", "py"), None),
            P(None, ("px", "py")),
            P(None, ("px", "py")),
        ),
        out_specs=P(None, None, "px", "py"),
        check_vma=False,
    )
```
